32 devices in a mesh: dp: 8 (over y, x, core), mp: 4 (over z).
Axes of the slice: x: 2, y: 2, z: 4, core: 2. Of those that a mesh axis runs over, the one named last changes fastest.
Arguments:
- series: bfloat16 [8, 512, 16, 256], P('dp', 'mp'), may hold values from -6 to 6
- upstream_grad: bfloat16 [8, 512, 16, 256], P('dp', None, 'mp'), may hold values from -3 to 3
- time_weights: bfloat16 [4, 256, 256], replicated, may hold values from -0.375 to 0.375
- channel_weights: bfloat16 [4, 256, 256], replicated, may hold values from -0.375 to 0.375
- neighbors: int32 [4, 3], replicated, may hold values from 0 to 3, as said below
Outputs:
- mixed_series: bfloat16 [8, 512, 16, 256], P('dp', None, 'mp')
- series_grad: bfloat16 [8, 512, 16, 256], P('dp', 'mp')
- time_grads: float32 [4, 256, 256], P(None, 'mp')
- channel_grads: float32 [4, 256, 256], P(None, 'mp')
The draws below stay inside these ranges and needn't reach their ends.
Inputs may be any that keep to these rules, and one draw needn't show every extreme that they name: `neighbors`: row b names 3 different blocks; its first entry is b.
All inputs are finite; a program needn't handle non-finite values.
Results may differ from the reference program's by a relative error of at most 0.025.
Values may be sent and summed in bfloat16 or wider, within the bound.
A program may use at most 192 MiB of HBM per device.

```python
import jax
import jax.numpy as jnp
from jax import lax

D = 256
HEADS = 4
NBR = 3
L = 16
B = 8
C = 512
BLOCKS = 4


def draw_neighbors(key, part):
    attention_logits = jax.random.randint(key, (BLOCKS, BLOCKS), 0, 4096, dtype=jnp.int32)
    columns = jnp.arange(BLOCKS, dtype=jnp.int32)
    attention_logits = attention_logits * BLOCKS + columns[None, :]
    attention_logits = jnp.where(columns[None, :] == columns[:, None], jnp.int32(1 << 30), attention_logits)
    order = jnp.argsort(attention_logits, axis=1, stable=True).astype(jnp.int32)
    return jnp.concatenate([columns[:, None], order[:, :NBR - 1]], axis=1).astype(jnp.int32)


def level_of(key, shape, split, smallest, largest):
    gain = 1.0
    for axis_at, blocks in split:
        steps = jax.random.uniform(jax.random.fold_in(jax.random.fold_in(key, 6), axis_at), (blocks,), jnp.float32, smallest / len(split), largest / len(split))
        gain = gain * jnp.repeat(jnp.exp(steps), shape[axis_at] // blocks).reshape((-1,) + (1,) * (len(shape) - 1 - axis_at))
    return gain


def normal_values(rng, extent, spread, limit, cuts=(), held_as=jnp.bfloat16):
    entries = spread * jax.random.normal(rng, extent, jnp.float32)
    if cuts:
        entries = entries * level_of(rng, extent, cuts, -0.22, 0.18)
    return jnp.clip(entries, -limit, limit).astype(held_as)


def setup_inputs(seed: int = 0) -> dict:
    key_list = jax.random.split(jax.random.key(seed), 6)
    return {
        "series": normal_values(key_list[0], (B, C, L, D), 1.0, 6.0, ((0, 8), (1, 4))),
        "upstream_grad": normal_values(key_list[1], (B, C, L, D), 0.5, 3.0, ((0, 8), (2, 4))),
        "time_weights": normal_values(key_list[2], (4, D, D), D ** -0.5, 0.375),
        "channel_weights": normal_values(key_list[3], (4, D, D), D ** -0.5, 0.375),
        "neighbors": draw_neighbors(jax.random.fold_in(key_list[5], 71), 0),
    }


EPS = 1e-06
LOGIT_SCALE = 0.25

def cast_to_single_float(values):
    return values.astype(jnp.float32)

def cast_to_brain_float(values):
    return lax.optimization_barrier(values.astype(jnp.bfloat16))

def row_norm(inputs):
    return inputs * lax.rsqrt(lax.optimization_barrier(jnp.mean(inputs * inputs, axis=-1, keepdims=True)) + EPS)

def head_norm(inputs):
    shaped = inputs.reshape(inputs.shape[:-1] + (HEADS, inputs.shape[-1] // HEADS))
    return row_norm(shaped).reshape(inputs.shape)

def project(normed, weights):
    raw_query = jnp.dot(normed, weights[0], preferred_element_type=jnp.float32)
    raw_key = jnp.dot(normed, weights[1], preferred_element_type=jnp.float32)
    value_rows = cast_to_brain_float(jnp.dot(normed, weights[2], preferred_element_type=jnp.float32))
    query_rows = cast_to_brain_float(head_norm(raw_query))
    key_rows = cast_to_brain_float(head_norm(raw_key))
    return (raw_query, raw_key, query_rows, key_rows, value_rows)

def project_back(normed, raw_query, raw_key, query_grad, key_grad, value_grad, weights):
    query_back = cast_to_brain_float(jax.vjp(head_norm, raw_query)[1](query_grad)[0])
    key_back = cast_to_brain_float(jax.vjp(head_norm, raw_key)[1](key_grad)[0])
    value_back = cast_to_brain_float(value_grad)
    weight_grads = [jnp.dot(normed.T, back_rows, preferred_element_type=jnp.float32) for back_rows in (query_back, key_back, value_back)]
    normed_grad = jnp.dot(query_back, weights[0].T, preferred_element_type=jnp.float32)
    normed_grad = normed_grad + jnp.dot(key_back, weights[1].T, preferred_element_type=jnp.float32)
    normed_grad = normed_grad + jnp.dot(value_back, weights[2].T, preferred_element_type=jnp.float32)
    return (normed_grad, weight_grads)

def attend_time(query_heads, key_heads, value_heads):
    attention_logits = LOGIT_SCALE * jnp.einsum('clhe,cmhe->hlmc', cast_to_single_float(query_heads), cast_to_single_float(key_heads))
    exponent = jnp.exp(attention_logits)
    attention_layer = exponent / lax.optimization_barrier(jnp.sum(exponent, axis=2, keepdims=True))
    weights_brain_float = cast_to_brain_float(attention_layer)
    mixed_heads = jnp.einsum('hlmc,cmhe->clhe', cast_to_single_float(weights_brain_float), cast_to_single_float(value_heads))
    return (cast_to_brain_float(mixed_heads), attention_layer)

def revert_time(query_heads, key_heads, value_heads, attention_layer, grad_heads):
    weights_brain_float = cast_to_brain_float(attention_layer)
    attention_gradient = jnp.einsum('clhe,cmhe->hlmc', cast_to_single_float(grad_heads), cast_to_single_float(value_heads))
    row_delta = lax.optimization_barrier(jnp.sum(attention_layer * attention_gradient, axis=2, keepdims=True))
    logit_gradient = cast_to_brain_float(LOGIT_SCALE * attention_layer * (attention_gradient - row_delta))
    query_grad = jnp.einsum('hlmc,cmhe->clhe', cast_to_single_float(logit_gradient), cast_to_single_float(key_heads))
    key_grad = jnp.einsum('hlmc,clhe->cmhe', cast_to_single_float(logit_gradient), cast_to_single_float(query_heads))
    value_grad = jnp.einsum('hlmc,clhe->cmhe', cast_to_single_float(weights_brain_float), cast_to_single_float(grad_heads))
    return (query_grad, key_grad, value_grad)

def forward_time(series_rows, weights):
    channel_count, length, features = series_rows.shape
    total_rows = channel_count * length
    normed = cast_to_brain_float(row_norm(cast_to_single_float(series_rows))).reshape(total_rows, features)
    raw_query, raw_key, query_rows, key_rows, value_rows = project(normed, weights)
    shaped = (channel_count, length, HEADS, features // HEADS)
    mixed_heads, attention_layer = attend_time(query_rows.reshape(shaped), key_rows.reshape(shaped), value_rows.reshape(shaped))
    mixed_flat = mixed_heads.reshape(total_rows, features)
    branch = jnp.dot(mixed_flat, weights[3], preferred_element_type=jnp.float32).reshape(series_rows.shape)
    stream = cast_to_brain_float(cast_to_single_float(series_rows) + branch)
    return (stream, (normed, raw_query, raw_key, query_rows, key_rows, value_rows, mixed_flat, attention_layer))

def backward_time(series_rows, stored, stream_grad, weights):
    normed, raw_query, raw_key, query_rows, key_rows, value_rows, mixed_flat, attention_layer = stored
    channel_count, length, features = series_rows.shape
    total_rows = channel_count * length
    shaped = (channel_count, length, HEADS, features // HEADS)
    grad_flat = stream_grad.reshape(total_rows, features)
    out_grad = jnp.dot(mixed_flat.T, grad_flat, preferred_element_type=jnp.float32)
    mixed_grad = cast_to_brain_float(jnp.dot(grad_flat, weights[3].T, preferred_element_type=jnp.float32))
    query_grad, key_grad, value_grad = revert_time(query_rows.reshape(shaped), key_rows.reshape(shaped), value_rows.reshape(shaped), attention_layer, mixed_grad.reshape(shaped))
    normed_grad, weight_grads = project_back(normed, raw_query, raw_key, query_grad.reshape(total_rows, features), key_grad.reshape(total_rows, features), value_grad.reshape(total_rows, features), weights)
    norm_back = jax.vjp(row_norm, cast_to_single_float(series_rows))[1]
    series_grad = cast_to_brain_float(cast_to_single_float(stream_grad) + norm_back(normed_grad.reshape(series_rows.shape))[0])
    return (series_grad, jnp.stack(weight_grads + [out_grad]))

def near_blocks(source_rows, neighbors):
    block_list = neighbors.shape[0]
    shaped = source_rows.reshape(block_list, source_rows.shape[0] // block_list, source_rows.shape[1])
    return shaped[neighbors].reshape(block_list, -1, source_rows.shape[1])

def attend_channels(query_rows, key_rows, value_rows, neighbors):
    block_list = neighbors.shape[0]
    features = query_rows.shape[1]
    head_width = features // HEADS
    query_blocks = query_rows.reshape(block_list, -1, features)
    key_near = near_blocks(key_rows, neighbors)
    value_near = near_blocks(value_rows, neighbors)
    per_head_output = []
    for head_number in range(HEADS):
        first_col = head_number * head_width
        single_query_head = query_blocks[:, :, first_col:first_col + head_width]
        single_key_head = key_near[:, :, first_col:first_col + head_width]
        single_value_head = value_near[:, :, first_col:first_col + head_width]
        attention_logits = LOGIT_SCALE * jnp.einsum('fdr,fwr->fdw', cast_to_single_float(single_query_head), cast_to_single_float(single_key_head))
        exponent = jnp.exp(attention_logits)
        attention_layer = exponent / lax.optimization_barrier(jnp.sum(exponent, axis=2, keepdims=True))
        per_head_output.append(jnp.einsum('xlj,xjr->xlr', cast_to_single_float(cast_to_brain_float(attention_layer)), cast_to_single_float(single_value_head)))
    return cast_to_brain_float(jnp.concatenate(per_head_output, axis=2).reshape(query_rows.shape))

def join_heads(head_parts, shape):
    return jnp.concatenate(head_parts, axis=2).reshape(shape)

def revert_channels(query_rows, key_rows, value_rows, neighbors, mixed_grad):
    block_list, neighbor_count = neighbors.shape
    features = query_rows.shape[1]
    head_width = features // HEADS
    block_length = query_rows.shape[0] // block_list
    onehot = (neighbors.reshape(-1)[:, None] == jnp.arange(block_list, dtype=jnp.int32)[None, :]).astype(jnp.float32)
    query_blocks = query_rows.reshape(block_list, -1, features)
    grad_blocks = mixed_grad.reshape(block_list, -1, features)
    key_near = near_blocks(key_rows, neighbors)
    value_near = near_blocks(value_rows, neighbors)
    query_pieces_list, key_parts, value_parts = ([], [], [])
    for head_number in range(HEADS):
        first_col = head_number * head_width
        single_query_head = query_blocks[:, :, first_col:first_col + head_width]
        single_key_head = key_near[:, :, first_col:first_col + head_width]
        single_value_head = value_near[:, :, first_col:first_col + head_width]
        head_gradient = grad_blocks[:, :, first_col:first_col + head_width]
        attention_logits = LOGIT_SCALE * jnp.einsum('fdr,fwr->fdw', cast_to_single_float(single_query_head), cast_to_single_float(single_key_head))
        exponent = jnp.exp(attention_logits)
        attention_layer = exponent / lax.optimization_barrier(jnp.sum(exponent, axis=2, keepdims=True))
        weights_brain_float = cast_to_brain_float(attention_layer)
        attention_gradient = jnp.einsum('fdr,fwr->fdw', cast_to_single_float(head_gradient), cast_to_single_float(single_value_head))
        row_delta = lax.optimization_barrier(jnp.sum(attention_layer * attention_gradient, axis=2, keepdims=True))
        logit_gradient = cast_to_brain_float(LOGIT_SCALE * attention_layer * (attention_gradient - row_delta))
        query_pieces_list.append(jnp.einsum('xlj,xjr->xlr', cast_to_single_float(logit_gradient), cast_to_single_float(single_key_head)))
        neighbor_key_gradient = jnp.einsum('tsa,tsg->tag', cast_to_single_float(logit_gradient), cast_to_single_float(single_query_head)).reshape(block_list * neighbor_count, block_length, head_width)
        neighbor_value_gradient = jnp.einsum('tsa,tsg->tag', cast_to_single_float(weights_brain_float), cast_to_single_float(head_gradient)).reshape(block_list * neighbor_count, block_length, head_width)
        key_parts.append(jnp.einsum('ob,ote->bte', onehot, neighbor_key_gradient, precision=lax.Precision.HIGHEST))
        value_parts.append(jnp.einsum('ob,ote->bte', onehot, neighbor_value_gradient, precision=lax.Precision.HIGHEST))
    shape = query_rows.shape
    return (join_heads(query_pieces_list, shape), join_heads(key_parts, shape), join_heads(value_parts, shape))

def forward_channels(stream_rows, weights, neighbors):
    stream_float = cast_to_single_float(stream_rows)
    normed = cast_to_brain_float(row_norm(stream_float))
    raw_query, raw_key, query_rows, key_rows, value_rows = project(normed, weights)
    mixed_rows = attend_channels(query_rows, key_rows, value_rows, neighbors)
    output_rows = cast_to_brain_float(stream_float + jnp.dot(mixed_rows, weights[3], preferred_element_type=jnp.float32))
    return (output_rows, normed, raw_query, raw_key, value_rows, mixed_rows)

def backward_channels(stream_rows, normed, raw_query, raw_key, value_rows, mixed_rows, upstream_rows, weights, neighbors):
    out_grad = jnp.dot(mixed_rows.T, upstream_rows, preferred_element_type=jnp.float32)
    mixed_grad = cast_to_brain_float(jnp.dot(upstream_rows, weights[3].T, preferred_element_type=jnp.float32))
    query_rows = cast_to_brain_float(head_norm(raw_query))
    key_rows = cast_to_brain_float(head_norm(raw_key))
    query_grad, key_grad, value_grad = revert_channels(query_rows, key_rows, value_rows, neighbors, mixed_grad)
    normed_grad, weight_grads = project_back(normed, raw_query, raw_key, query_grad, key_grad, value_grad, weights)
    norm_back = jax.vjp(row_norm, cast_to_single_float(stream_rows))[1]
    stream_grad = cast_to_brain_float(cast_to_single_float(upstream_rows) + norm_back(normed_grad)[0])
    return (stream_grad, jnp.stack(weight_grads + [out_grad]))

def reference(series, upstream_grad, time_weights, channel_weights, neighbors):

    def sample_pass(sample_pair):
        series_rows, upstream_rows = sample_pair
        stream, stored = forward_time(series_rows, time_weights)

        def segment_pass(segment_pair):
            stream_seg, upstream_seg = segment_pair
            output_rows, normed, raw_query, raw_key, value_rows, mixed_rows = forward_channels(stream_seg, channel_weights, neighbors)
            stream_grad, grad_stack = backward_channels(stream_seg, normed, raw_query, raw_key, value_rows, mixed_rows, upstream_seg, channel_weights, neighbors)
            return (output_rows, stream_grad, grad_stack)
        outputs, stream_grads, channel_parts = lax.map(segment_pass, (jnp.swapaxes(stream, 0, 1), jnp.swapaxes(upstream_rows, 0, 1)))
        series_grad, time_part = backward_time(series_rows, stored, jnp.swapaxes(stream_grads, 0, 1), time_weights)
        return (jnp.swapaxes(outputs, 0, 1), series_grad, time_part, lax.optimization_barrier(jnp.sum(channel_parts, axis=0)))
    mixed_series, series_grad, time_parts, channel_parts = lax.map(sample_pass, (series, upstream_grad))
    time_grads = lax.optimization_barrier(jnp.sum(time_parts, axis=0)) / B
    channel_grads = lax.optimization_barrier(jnp.sum(channel_parts, axis=0)) / B
    return (mixed_series, series_grad, time_grads, channel_grads)
```

```python
import functools

import jax
import jax.numpy as jnp
from jax import lax
from jax.experimental import pallas as pl
from jax.experimental.pallas import tpu as pltpu
from jax.sharding import PartitionSpec as P

HEADS = 4
EPS = 1e-06
LOGIT_SCALE = 0.25
GROUP = 128

F32 = jnp.float32
BF16 = jnp.bfloat16


def mm(a, b):
    return lax.dot_general(a, b, (((1,), (0,)), ((), ())), preferred_element_type=F32)


def mm_nt(a, b):
    return lax.dot_general(a, b, (((1,), (1,)), ((), ())), preferred_element_type=F32)


def mm_tn(a, b):
    return lax.dot_general(a, b, (((0,), (0,)), ((), ())), preferred_element_type=F32)


def head_blocks(features):
    width = features // HEADS
    rows = lax.broadcasted_iota(jnp.int32, (features, features), 0) // width
    cols = lax.broadcasted_iota(jnp.int32, (features, features), 1) // width
    return jnp.where(rows == cols, 1.0 / width, 0.0).astype(BF16)


def head_mean(values, blocks):
    high = values.astype(BF16)
    low = (values - high.astype(F32)).astype(BF16)
    return mm(high, blocks) + mm(low, blocks)


def inv_rms(values):
    return lax.rsqrt(jnp.mean(values * values, axis=-1, keepdims=True) + EPS)


def head_hat(raw, blocks):
    inv = lax.rsqrt(head_mean(raw * raw, blocks) + EPS)
    return raw * inv, inv


def head_back(raw, grad, blocks):
    hat, inv = head_hat(raw, blocks)
    return inv * (grad - hat * head_mean(hat * grad, blocks))


def row_back(rows, grad):
    inv = inv_rms(rows)
    hat = rows * inv
    return inv * (grad - hat * jnp.mean(hat * grad, axis=-1, keepdims=True))


def head_of_lane(shape):
    return lax.broadcasted_iota(jnp.int32, shape, 1) // (shape[1] // HEADS)


def stack_heads(rows):
    lane_head = head_of_lane(rows.shape)
    wide = rows.astype(F32)
    return jnp.concatenate(
        [jnp.where(lane_head == h, wide, 0.0).astype(BF16) for h in range(HEADS)], axis=0
    )


def pick_heads(stacked):
    count = stacked.shape[0] // HEADS
    lane_head = head_of_lane((count, stacked.shape[1]))
    out = stacked[:count]
    for h in range(1, HEADS):
        out = jnp.where(lane_head == h, stacked[h * count : (h + 1) * count], out)
    return out


def softmax_rows(q_stack, keys, keep):
    exponent = jnp.exp(LOGIT_SCALE * mm_nt(q_stack, keys))
    if keep is not None:
        exponent = exponent * keep
    return exponent * (1.0 / jnp.sum(exponent, axis=-1, keepdims=True))


def score_grads(attention, g_stack, values):
    grad = mm_nt(g_stack, values)
    delta = jnp.sum(attention * grad, axis=-1, keepdims=True)
    return (LOGIT_SCALE * attention * (grad - delta)).astype(BF16)


def same_channel(length):
    shape = (HEADS * GROUP, GROUP)
    rows = lax.rem(lax.broadcasted_iota(jnp.int32, shape, 0), GROUP) // length
    cols = lax.broadcasted_iota(jnp.int32, shape, 1) // length
    return jnp.where(rows == cols, 1.0, 0.0).astype(F32)


def project(normed, w_ref, blocks):
    raw_query = mm(normed, w_ref[0])
    raw_key = mm(normed, w_ref[1])
    value = mm(normed, w_ref[2]).astype(BF16)
    query = head_hat(raw_query, blocks)[0].astype(BF16)
    key = head_hat(raw_key, blocks)[0].astype(BF16)
    return raw_query, raw_key, query, key, value


def time_forward_kernel(length, x_ref, w_ref, out_ref, mixed_s, rows_s):
    rows = x_ref.shape[0]
    blocks = head_blocks(x_ref.shape[1])
    keep = same_channel(length)
    x = x_ref[...].astype(F32)
    normed = (x * inv_rms(x)).astype(BF16)
    _, _, query, key, value = project(normed, w_ref, blocks)
    for start in range(0, rows, GROUP):
        sl = slice(start, start + GROUP)
        weights = softmax_rows(stack_heads(query[sl]), key[sl], keep).astype(BF16)
        mixed_s[sl, :] = pick_heads(mm(weights, value[sl])).astype(BF16)
    stream = x + mm(mixed_s[...], w_ref[3])
    count = rows // length
    half = x_ref.shape[1] // 2
    for part in range(2):
        rows_s[part] = stream[:, part * half : (part + 1) * half]
    for seg in range(length):
        for part in range(2):
            out_ref[seg, :, part * half : (part + 1) * half] = rows_s[
                part, pl.ds(seg, count, stride=length), :
            ].astype(BF16)


def time_backward_kernel(
    length, x_ref, sg_ref, w_ref, out_ref, wg_ref, mixed_s, dq_s, dk_s, dv_s, rows_s
):
    rows, features = x_ref.shape
    count = rows // length
    half = features // 2
    blocks = head_blocks(features)
    keep = same_channel(length)
    for seg in range(length):
        for part in range(2):
            rows_s[part, pl.ds(seg, count, stride=length), :] = sg_ref[
                seg, :, part * half : (part + 1) * half
            ].astype(F32)
    up = jnp.concatenate([rows_s[0], rows_s[1]], axis=1)
    up_b = up.astype(BF16)
    x = x_ref[...].astype(F32)
    normed = (x * inv_rms(x)).astype(BF16)
    raw_query, raw_key, query, key, value = project(normed, w_ref, blocks)
    mixed_grad = mm_nt(up_b, w_ref[3]).astype(BF16)
    for start in range(0, rows, GROUP):
        sl = slice(start, start + GROUP)
        q_stack = stack_heads(query[sl])
        g_stack = stack_heads(mixed_grad[sl])
        attention = softmax_rows(q_stack, key[sl], keep)
        weights = attention.astype(BF16)
        mixed_s[sl, :] = pick_heads(mm(weights, value[sl])).astype(BF16)
        grads = score_grads(attention, g_stack, value[sl])
        dq_s[sl, :] = pick_heads(mm(grads, key[sl]))
        dk_s[sl, :] = mm_tn(grads, q_stack)
        dv_s[sl, :] = mm_tn(weights, g_stack)
    finish_backward(
        x, up, up_b, normed, raw_query, raw_key, mixed_s, dq_s, dk_s, dv_s, w_ref, wg_ref, blocks,
        out_ref,
    )


def finish_backward(
    x, up, up_b, normed, raw_query, raw_key, mixed_s, dq_s, dk_s, dv_s, w_ref, wg_ref, blocks, out_ref
):
    query_back = head_back(raw_query, dq_s[...], blocks).astype(BF16)
    key_back = head_back(raw_key, dk_s[...], blocks).astype(BF16)
    value_back = dv_s[...].astype(BF16)

    @pl.when(pl.program_id(0) == 0)
    def _():
        wg_ref[...] = jnp.zeros_like(wg_ref)

    wg_ref[0] += mm_tn(normed, query_back)
    wg_ref[1] += mm_tn(normed, key_back)
    wg_ref[2] += mm_tn(normed, value_back)
    wg_ref[3] += mm_tn(mixed_s[...], up_b)
    grad = mm_nt(query_back, w_ref[0]) + mm_nt(key_back, w_ref[1]) + mm_nt(value_back, w_ref[2])
    result = (up + row_back(x, grad)).astype(BF16)
    out_ref[...] = result.reshape(out_ref.shape)


def channel_kernel(
    near, nbr_ref, x_ref, up_ref, w_ref, out_ref, sg_ref, wg_ref,
    q_s, k_s, v_s, g_s, mixed_s, dq_s, dk_s, dv_s,
):
    channels, features = q_s.shape
    block = channels // nbr_ref.shape[0]
    blocks = head_blocks(features)
    x = x_ref[...].reshape(channels, features).astype(F32)
    normed = (x * inv_rms(x)).astype(BF16)
    raw_query, raw_key, query, key, value = project(normed, w_ref, blocks)
    q_s[...] = query
    k_s[...] = key
    v_s[...] = value
    up_b = up_ref[...].reshape(channels, features)
    g_s[...] = mm_nt(up_b, w_ref[3]).astype(BF16)
    dk_s[...] = jnp.zeros_like(dk_s)
    dv_s[...] = jnp.zeros_like(dv_s)

    def one_block(i, carry):
        mine = pl.ds(pl.multiple_of(i * block, block), block)
        theirs = [
            pl.ds(pl.multiple_of(nbr_ref[i, n] * block, block), block) for n in range(near)
        ]
        q_stack = stack_heads(q_s[mine, :])
        g_stack = stack_heads(g_s[mine, :])
        keys = jnp.concatenate([k_s[t, :] for t in theirs], axis=0)
        values = jnp.concatenate([v_s[t, :] for t in theirs], axis=0)
        attention = softmax_rows(q_stack, keys, None)
        weights = attention.astype(BF16)
        mixed_s[mine, :] = pick_heads(mm(weights, values)).astype(BF16)
        grads = score_grads(attention, g_stack, values)
        dq_s[mine, :] = pick_heads(mm(grads, keys))
        key_grad = mm_tn(grads, q_stack)
        value_grad = mm_tn(weights, g_stack)
        for n, t in enumerate(theirs):
            dk_s[t, :] += key_grad[n * block : (n + 1) * block]
            dv_s[t, :] += value_grad[n * block : (n + 1) * block]
        return carry

    lax.fori_loop(0, nbr_ref.shape[0], one_block, 0)
    out_ref[...] = (x + mm(mixed_s[...], w_ref[3])).astype(BF16).reshape(out_ref.shape)
    finish_backward(
        x, up_b.astype(F32), up_b, normed, raw_query, raw_key, mixed_s, dq_s, dk_s, dv_s, w_ref,
        wg_ref, blocks, sg_ref,
    )


VMEM_LIMIT = 56 * 1024 * 1024


def forward_time(rows, weights, length, step):
    total, features = rows.shape
    count = step // length
    return pl.pallas_call(
        functools.partial(time_forward_kernel, length),
        out_shape=jax.ShapeDtypeStruct((length, total // length, features), BF16),
        grid=(total // step,),
        in_specs=[
            pl.BlockSpec((step, features), lambda i: (i, 0)),
            pl.BlockSpec(weights.shape, lambda i: (0, 0, 0)),
        ],
        out_specs=pl.BlockSpec((length, count, features), lambda i: (0, i, 0)),
        scratch_shapes=[
            pltpu.VMEM((step, features), BF16),
            pltpu.VMEM((2, step, features // 2), F32),
        ],
        compiler_params=pltpu.CompilerParams(vmem_limit_bytes=VMEM_LIMIT),
        name="time_forward",
    )(rows, weights)


def backward_time(rows, grads, weights, length, step):
    total, features = rows.shape
    count = step // length
    return pl.pallas_call(
        functools.partial(time_backward_kernel, length),
        out_shape=(
            jax.ShapeDtypeStruct((total, features), BF16),
            jax.ShapeDtypeStruct(weights.shape, F32),
        ),
        grid=(total // step,),
        in_specs=[
            pl.BlockSpec((step, features), lambda i: (i, 0)),
            pl.BlockSpec((length, count, features), lambda i: (0, i, 0)),
            pl.BlockSpec(weights.shape, lambda i: (0, 0, 0)),
        ],
        out_specs=(
            pl.BlockSpec((step, features), lambda i: (i, 0)),
            pl.BlockSpec(weights.shape, lambda i: (0, 0, 0)),
        ),
        scratch_shapes=[pltpu.VMEM((step, features), BF16)]
        + [pltpu.VMEM((step, features), F32)] * 3
        + [pltpu.VMEM((2, step, features // 2), F32)],
        compiler_params=pltpu.CompilerParams(vmem_limit_bytes=VMEM_LIMIT),
        name="time_backward",
    )(rows, grads, weights)


def channel_layer(columns, upstream, weights, neighbors):
    parts, segments, own, features = columns.shape
    channels = parts * own
    seg_block = pl.BlockSpec((parts, 1, own, features), lambda i: (0, i, 0, 0))
    row_block = pl.BlockSpec((1, channels, features), lambda i: (i, 0, 0))
    w_block = pl.BlockSpec(weights.shape, lambda i: (0, 0, 0))
    return pl.pallas_call(
        functools.partial(channel_kernel, neighbors.shape[1]),
        out_shape=(
            jax.ShapeDtypeStruct(upstream.shape, BF16),
            jax.ShapeDtypeStruct(columns.shape, BF16),
            jax.ShapeDtypeStruct(weights.shape, F32),
        ),
        grid=(segments,),
        in_specs=[pl.BlockSpec(memory_space=pltpu.SMEM), seg_block, row_block, w_block],
        out_specs=(row_block, seg_block, w_block),
        scratch_shapes=[pltpu.VMEM((channels, features), BF16)] * 5
        + [pltpu.VMEM((channels, features), F32)] * 3,
        compiler_params=pltpu.CompilerParams(vmem_limit_bytes=VMEM_LIMIT),
        name="channel_layer",
    )(neighbors, columns, upstream, weights)


def reduce_grads(partial_sum):
    mine = lax.psum_scatter(partial_sum.astype(BF16), "mp", scatter_dimension=1, tiled=True)
    return lax.psum(mine, "dp").astype(F32)


def shards(series, upstream_grad, time_weights, channel_weights, neighbors):
    model_size = lax.axis_size("mp")
    data_size = lax.axis_size("dp")
    own, length, features = series.shape[1:]
    seg_count = length // model_size
    rows = series.reshape(own * length, features)
    step = min(own * length, 512)
    upstream = jnp.swapaxes(upstream_grad[0], 0, 1)
    stream = forward_time(rows, time_weights, length, step)
    columns = lax.all_to_all(
        stream.reshape(model_size, seg_count, own, features), "mp", split_axis=0, concat_axis=0
    )
    output, stream_grad, channel_part = channel_layer(columns, upstream, channel_weights, neighbors)
    returned = lax.all_to_all(stream_grad, "mp", split_axis=0, concat_axis=0)
    channel_grads = reduce_grads(channel_part) / data_size
    series_grad, time_part = backward_time(
        rows, returned.reshape(length, own, features), time_weights, length, step
    )
    time_grads = reduce_grads(time_part) / data_size
    return (
        jnp.swapaxes(output, 0, 1)[None],
        series_grad.reshape(series.shape),
        time_grads,
        channel_grads,
    )


def solution(mesh):
    placed = (P("dp", "mp", None, None), P("dp", None, "mp", None), P(), P(), P())
    return jax.shard_map(
        shards,
        mesh=mesh,
        in_specs=placed,
        out_specs=(
            P("dp", None, "mp", None),
            P("dp", "mp", None, None),
            P(None, "mp", None),
            P(None, "mp", None),
        ),
        check_vma=False,
    )
```

```python
import functools

import jax
import jax.numpy as jnp
from jax import lax
from jax.experimental import pallas as pl
from jax.experimental.pallas import tpu as pltpu
from jax.sharding import PartitionSpec as P

HEADS = 4
EPS = 1e-06
LOGIT_SCALE = 0.25
GROUP = 128

F32 = jnp.float32
BF16 = jnp.bfloat16
MESH = pl.DeviceIdType.MESH


def mm(a, b):
    return lax.dot_general(a, b, (((1,), (0,)), ((), ())), preferred_element_type=F32)


def mm_nt(a, b):
    return lax.dot_general(a, b, (((1,), (1,)), ((), ())), preferred_element_type=F32)


def mm_tn(a, b):
    return lax.dot_general(a, b, (((0,), (0,)), ((), ())), preferred_element_type=F32)


def head_blocks(features):
    width = features // HEADS
    rows = lax.broadcasted_iota(jnp.int32, (features, features), 0) // width
    cols = lax.broadcasted_iota(jnp.int32, (features, features), 1) // width
    return jnp.where(rows == cols, 1.0 / width, 0.0).astype(BF16)


def head_mean(values, blocks):
    high = values.astype(BF16)
    low = (values - high.astype(F32)).astype(BF16)
    return mm(high, blocks) + mm(low, blocks)


def inv_rms(values):
    return lax.rsqrt(jnp.mean(values * values, axis=-1, keepdims=True) + EPS)


def head_hat(raw, blocks):
    inv = lax.rsqrt(head_mean(raw * raw, blocks) + EPS)
    return raw * inv, inv


def head_back(raw, grad, blocks):
    hat, inv = head_hat(raw, blocks)
    return inv * (grad - hat * head_mean(hat * grad, blocks))


def row_back(rows, grad):
    inv = inv_rms(rows)
    hat = rows * inv
    return inv * (grad - hat * jnp.mean(hat * grad, axis=-1, keepdims=True))


def head_of_lane(shape):
    return lax.broadcasted_iota(jnp.int32, shape, 1) // (shape[1] // HEADS)


def stack_heads(rows):
    lane_head = head_of_lane(rows.shape)
    wide = rows.astype(F32)
    return jnp.concatenate(
        [jnp.where(lane_head == h, wide, 0.0).astype(BF16) for h in range(HEADS)], axis=0
    )


def pick_heads(stacked):
    count = stacked.shape[0] // HEADS
    lane_head = head_of_lane((count, stacked.shape[1]))
    out = stacked[:count]
    for h in range(1, HEADS):
        out = jnp.where(lane_head == h, stacked[h * count : (h + 1) * count], out)
    return out


def softmax_rows(q_stack, keys, keep):
    exponent = jnp.exp(LOGIT_SCALE * mm_nt(q_stack, keys))
    if keep is not None:
        exponent = exponent * keep
    return exponent * (1.0 / jnp.sum(exponent, axis=-1, keepdims=True))


def score_grads(attention, g_stack, values):
    grad = mm_nt(g_stack, values)
    delta = jnp.sum(attention * grad, axis=-1, keepdims=True)
    return (LOGIT_SCALE * attention * (grad - delta)).astype(BF16)


def same_channel(length):
    shape = (HEADS * GROUP, GROUP)
    rows = lax.rem(lax.broadcasted_iota(jnp.int32, shape, 0), GROUP) // length
    cols = lax.broadcasted_iota(jnp.int32, shape, 1) // length
    return jnp.where(rows == cols, 1.0, 0.0).astype(F32)


def project(normed, w_ref, blocks):
    raw_query = mm(normed, w_ref[0])
    raw_key = mm(normed, w_ref[1])
    value = mm(normed, w_ref[2]).astype(BF16)
    query = head_hat(raw_query, blocks)[0].astype(BF16)
    key = head_hat(raw_key, blocks)[0].astype(BF16)
    return raw_query, raw_key, query, key, value


def time_forward_kernel(length, x_ref, w_ref, out_ref, mixed_s, rows_s):
    rows = x_ref.shape[0]
    blocks = head_blocks(x_ref.shape[1])
    keep = same_channel(length)
    x = x_ref[...].astype(F32)
    normed = (x * inv_rms(x)).astype(BF16)
    _, _, query, key, value = project(normed, w_ref, blocks)
    for start in range(0, rows, GROUP):
        sl = slice(start, start + GROUP)
        weights = softmax_rows(stack_heads(query[sl]), key[sl], keep).astype(BF16)
        mixed_s[sl, :] = pick_heads(mm(weights, value[sl])).astype(BF16)
    stream = x + mm(mixed_s[...], w_ref[3])
    count = rows // length
    half = x_ref.shape[1] // 2
    for part in range(2):
        rows_s[part] = stream[:, part * half : (part + 1) * half]
    for seg in range(length):
        for part in range(2):
            out_ref[seg, :, part * half : (part + 1) * half] = rows_s[
                part, pl.ds(seg, count, stride=length), :
            ].astype(BF16)


def time_backward_kernel(
    length, x_ref, sg_ref, w_ref, out_ref, wg_ref, mixed_s, dq_s, dk_s, dv_s, rows_s
):
    rows, features = x_ref.shape
    count = rows // length
    half = features // 2
    blocks = head_blocks(features)
    keep = same_channel(length)
    for seg in range(length):
        for part in range(2):
            rows_s[part, pl.ds(seg, count, stride=length), :] = sg_ref[
                seg, :, part * half : (part + 1) * half
            ].astype(F32)
    up = jnp.concatenate([rows_s[0], rows_s[1]], axis=1)
    up_b = up.astype(BF16)
    x = x_ref[...].astype(F32)
    normed = (x * inv_rms(x)).astype(BF16)
    raw_query, raw_key, query, key, value = project(normed, w_ref, blocks)
    mixed_grad = mm_nt(up_b, w_ref[3]).astype(BF16)
    for start in range(0, rows, GROUP):
        sl = slice(start, start + GROUP)
        q_stack = stack_heads(query[sl])
        g_stack = stack_heads(mixed_grad[sl])
        attention = softmax_rows(q_stack, key[sl], keep)
        weights = attention.astype(BF16)
        mixed_s[sl, :] = pick_heads(mm(weights, value[sl])).astype(BF16)
        grads = score_grads(attention, g_stack, value[sl])
        dq_s[sl, :] = pick_heads(mm(grads, key[sl]))
        dk_s[sl, :] = mm_tn(grads, q_stack)
        dv_s[sl, :] = mm_tn(weights, g_stack)

    @pl.when(pl.program_id(0) == 0)
    def _():
        wg_ref[...] = jnp.zeros_like(wg_ref)

    out_ref[...] = finish_backward(
        x, up, up_b, normed, raw_query, raw_key, mixed_s[...], dq_s, dk_s, dv_s, w_ref, wg_ref, blocks
    )


def finish_backward(
    x, up, up_b, normed, raw_query, raw_key, mixed, dq_s, dk_s, dv_s, w_ref, wg_ref, blocks
):
    query_back = head_back(raw_query, dq_s[...], blocks).astype(BF16)
    key_back = head_back(raw_key, dk_s[...], blocks).astype(BF16)
    value_back = dv_s[...].astype(BF16)
    wg_ref[0] += mm_tn(normed, query_back)
    wg_ref[1] += mm_tn(normed, key_back)
    wg_ref[2] += mm_tn(normed, value_back)
    wg_ref[3] += mm_tn(mixed, up_b)
    grad = mm_nt(query_back, w_ref[0]) + mm_nt(key_back, w_ref[1]) + mm_nt(value_back, w_ref[2])
    return (up + row_back(x, grad)).astype(BF16)


def greet(peers):
    barrier = pltpu.get_barrier_semaphore()
    for peer in peers:
        pl.semaphore_signal(barrier, inc=1, device_id=peer, device_id_type=MESH)
    pl.semaphore_wait(barrier, len(peers))


def others(axis, size):
    me = lax.axis_index(axis)
    return [lax.rem(me + k, size) for k in range(1, size)]


def channel_kernel(
    parts, keep_ref, stream_ref, up_ref, w_ref, out_ref, ret_ref, wg_ref,
    cols_s, sg_s, q_s, k_s, v_s, g_s, mixed_s, dq_s, dk_s, dv_s,
    in_send, in_recv, back_send, back_recv, own_sem,
):
    segments, channels, features = up_ref.shape
    block_count = keep_ref.shape[0]
    block = channels // block_count
    blocks = head_blocks(features)
    me = lax.axis_index("mp")
    peers = others("mp", parts)
    greet([{"mp": peer} for peer in peers])

    def inward(k, seg):
        return pltpu.make_async_remote_copy(
            src_ref=stream_ref.at[peers[k], seg],
            dst_ref=cols_s.at[me, seg],
            send_sem=in_send.at[k, seg],
            recv_sem=in_recv.at[k, seg],
            device_id={"mp": peers[k]},
            device_id_type=MESH,
        )

    def back(k, seg):
        return pltpu.make_async_remote_copy(
            src_ref=sg_s.at[peers[k], seg],
            dst_ref=ret_ref.at[me, seg],
            send_sem=back_send.at[k, seg],
            recv_sem=back_recv.at[k, seg],
            device_id={"mp": peers[k]},
            device_id_type=MESH,
        )

    def keep_own(seg):
        return pltpu.make_async_copy(sg_s.at[me, seg], ret_ref.at[me, seg], own_sem.at[seg])

    for seg in range(segments):
        for k in range(parts - 1):
            inward(k, seg).start()
    cols_s[me] = stream_ref[me]
    wg_ref[...] = jnp.zeros_like(wg_ref)

    def one_segment(seg, carry):
        up_b = up_ref[seg]
        g_s[...] = mm_nt(up_b, w_ref[3]).astype(BF16)
        for k in range(parts - 1):
            inward(k, seg).wait_recv()
        x = cols_s[:, seg].reshape(channels, features).astype(F32)
        normed = (x * inv_rms(x)).astype(BF16)
        raw_query, raw_key, query, key, value = project(normed, w_ref, blocks)
        q_s[...] = query
        k_s[...] = key
        v_s[...] = value

        dk_s[...] = jnp.zeros_like(dk_s)
        dv_s[...] = jnp.zeros_like(dv_s)

        def one_block(i, inner):
            mine = pl.ds(pl.multiple_of(i * block, block), block)
            q_stack = stack_heads(q_s[mine, :])
            g_stack = stack_heads(g_s[mine, :])
            attention = softmax_rows(q_stack, k_s[...], keep_ref[i])
            weights = attention.astype(BF16)
            mixed_s[mine, :] = pick_heads(mm(weights, v_s[...])).astype(BF16)
            grads = score_grads(attention, g_stack, v_s[...])
            dq_s[mine, :] = pick_heads(mm(grads, k_s[...]))
            dk_s[...] += mm_tn(grads, q_stack)
            dv_s[...] += mm_tn(weights, g_stack)
            return inner

        lax.fori_loop(0, block_count, one_block, 0)
        sg = finish_backward(
            x, up_b.astype(F32), up_b, normed, raw_query, raw_key, mixed_s[...], dq_s, dk_s, dv_s,
            w_ref, wg_ref, blocks,
        )
        sg_s[:, seg] = sg.reshape(parts, channels // parts, features)
        for k in range(parts - 1):
            back(k, seg).start()
        keep_own(seg).start()
        out_ref[seg] = (x + mm(mixed_s[...], w_ref[3])).astype(BF16)
        return carry

    lax.fori_loop(0, segments, one_segment, 0)
    for seg in range(segments):
        keep_own(seg).wait()
        for k in range(parts - 1):
            inward(k, seg).wait_send()
            back(k, seg).wait()


def reduce_kernel(
    dp, mp, time_ref, chan_ref, time_out, chan_out, all_s, dp_in, mp_mine, mp_in, done_s, done_in,
    send1, recv1, send2, recv2, send3, recv3,
):
    matrices = time_ref.shape[0]
    width = all_s.shape[2]
    splits = time_ref.shape[2] // width
    me_dp, me_mp = lax.axis_index("dp"), lax.axis_index("mp")
    dp_peers, mp_peers = others("dp", dp), others("mp", mp)
    greet([{"dp": peer} for peer in dp_peers] + [{"mp": peer} for peer in mp_peers])

    def exchange(src, dst, send, recv, k, device):
        return pltpu.make_async_remote_copy(
            src_ref=src, dst_ref=dst, send_sem=send.at[k], recv_sem=recv.at[k],
            device_id=device, device_id_type=MESH,
        )

    for source, ref in enumerate((time_ref, chan_ref)):
        for m in range(matrices):
            for part in range(splits):
                place = (source * matrices + m) * splits + part
                all_s[place] = ref[m, :, part * width : (part + 1) * width].astype(BF16)
    copies = [
        exchange(all_s.at[p], dp_in.at[k], send1, recv1, k, {"dp": p})
        for k, p in enumerate(dp_peers)
    ]
    for copy in copies:
        copy.start()
    for copy in copies:
        copy.wait()
    total = all_s[me_dp].astype(F32)
    for k in range(dp - 1):
        total = total + dp_in[k].astype(F32)
    mp_mine[...] = total.astype(BF16).reshape(mp_mine.shape)
    copies = [
        exchange(mp_mine.at[p], mp_in.at[k], send2, recv2, k, {"mp": p})
        for k, p in enumerate(mp_peers)
    ]
    for copy in copies:
        copy.start()
    for copy in copies:
        copy.wait()
    total = mp_mine[me_mp].astype(F32)
    for k in range(mp - 1):
        total = total + mp_in[k].astype(F32)
    done_s[...] = total.astype(BF16)
    copies = [
        exchange(done_s, done_in.at[me_dp], send3, recv3, k, {"dp": p})
        for k, p in enumerate(dp_peers)
    ]
    for copy in copies:
        copy.start()
    done_in[me_dp] = done_s[...]
    for copy in copies:
        copy.wait()
    for source, ref in enumerate((time_out, chan_out)):
        for m in range(matrices):
            for part in range(splits):
                place = (source * matrices + m) * splits + part
                ref[m, :, part * width : (part + 1) * width] = done_in[place].astype(F32) / dp


VMEM_LIMIT = 56 * 1024 * 1024


def forward_time(rows, weights, length, step):
    total, features = rows.shape
    count = step // length
    return pl.pallas_call(
        functools.partial(time_forward_kernel, length),
        out_shape=jax.ShapeDtypeStruct((length, total // length, features), BF16),
        grid=(total // step,),
        in_specs=[
            pl.BlockSpec((step, features), lambda i: (i, 0)),
            pl.BlockSpec(weights.shape, lambda i: (0, 0, 0)),
        ],
        out_specs=pl.BlockSpec((length, count, features), lambda i: (0, i, 0)),
        scratch_shapes=[
            pltpu.VMEM((step, features), BF16),
            pltpu.VMEM((2, step, features // 2), F32),
        ],
        compiler_params=pltpu.CompilerParams(vmem_limit_bytes=VMEM_LIMIT),
        name="time_forward",
    )(rows, weights)


def backward_time(rows, grads, weights, length, step):
    total, features = rows.shape
    count = step // length
    return pl.pallas_call(
        functools.partial(time_backward_kernel, length),
        out_shape=(
            jax.ShapeDtypeStruct((total, features), BF16),
            jax.ShapeDtypeStruct(weights.shape, F32),
        ),
        grid=(total // step,),
        in_specs=[
            pl.BlockSpec((step, features), lambda i: (i, 0)),
            pl.BlockSpec((length, count, features), lambda i: (0, i, 0)),
            pl.BlockSpec(weights.shape, lambda i: (0, 0, 0)),
        ],
        out_specs=(
            pl.BlockSpec((step, features), lambda i: (i, 0)),
            pl.BlockSpec(weights.shape, lambda i: (0, 0, 0)),
        ),
        scratch_shapes=[pltpu.VMEM((step, features), BF16)]
        + [pltpu.VMEM((step, features), F32)] * 3
        + [pltpu.VMEM((2, step, features // 2), F32)],
        compiler_params=pltpu.CompilerParams(vmem_limit_bytes=VMEM_LIMIT),
        name="time_backward",
    )(rows, grads, weights)


def channel_layer(stream, upstream, weights, neighbors):
    parts, segments, own, features = stream.shape
    channels = parts * own
    block_count = neighbors.shape[0]
    lane_block = jnp.arange(channels, dtype=jnp.int32) // (channels // block_count)
    keep = jnp.any(neighbors[:, :, None] == lane_block[None, None, :], axis=1, keepdims=True)
    vmem = pl.BlockSpec(memory_space=pltpu.VMEM)
    rows_b = pltpu.VMEM((channels, features), BF16)
    rows_f = pltpu.VMEM((channels, features), F32)
    pair_sems = pltpu.SemaphoreType.DMA((parts - 1, segments))
    return pl.pallas_call(
        functools.partial(channel_kernel, parts),
        out_shape=(
            jax.ShapeDtypeStruct(upstream.shape, BF16),
            jax.ShapeDtypeStruct(stream.shape, BF16),
            jax.ShapeDtypeStruct(weights.shape, F32),
        ),
        in_specs=[vmem] * 4,
        out_specs=(vmem, pl.BlockSpec(memory_space=pl.ANY), vmem),
        scratch_shapes=[pltpu.VMEM(stream.shape, BF16)] * 2
        + [rows_b] * 5
        + [rows_f] * 3
        + [pair_sems] * 4
        + [pltpu.SemaphoreType.DMA((segments,))],
        compiler_params=pltpu.CompilerParams(
            vmem_limit_bytes=VMEM_LIMIT, collective_id=0, has_side_effects=True
        ),
        name="channel_layer",
    )(keep.astype(F32), stream, upstream, weights)


def reduce_grads(time_part, channel_part):
    dp, mp = lax.axis_size("dp"), lax.axis_size("mp")
    matrices, rows, features = time_part.shape
    width = features * 2 * matrices // dp
    mine = rows // mp
    vmem = pl.BlockSpec(memory_space=pltpu.VMEM)
    out = jax.ShapeDtypeStruct((matrices, mine, features), F32)
    return pl.pallas_call(
        functools.partial(reduce_kernel, dp, mp),
        out_shape=(out, out),
        in_specs=[vmem, vmem],
        out_specs=(vmem, vmem),
        scratch_shapes=[
            pltpu.VMEM((dp, rows, width), BF16),
            pltpu.VMEM((dp - 1, rows, width), BF16),
            pltpu.VMEM((mp, mine, width), BF16),
            pltpu.VMEM((mp - 1, mine, width), BF16),
            pltpu.VMEM((mine, width), BF16),
            pltpu.VMEM((dp, mine, width), BF16),
        ]
        + [pltpu.SemaphoreType.DMA((dp - 1,))] * 2
        + [pltpu.SemaphoreType.DMA((mp - 1,))] * 2
        + [pltpu.SemaphoreType.DMA((dp - 1,))] * 2,
        compiler_params=pltpu.CompilerParams(
            vmem_limit_bytes=VMEM_LIMIT, collective_id=1, has_side_effects=True
        ),
        name="reduce_grads",
    )(time_part, channel_part)


def shards(series, upstream_grad, time_weights, channel_weights, neighbors):
    model_size = lax.axis_size("mp")
    own, length, features = series.shape[1:]
    seg_count = length // model_size
    rows = series.reshape(own * length, features)
    step = min(own * length, 512)
    upstream = jnp.swapaxes(upstream_grad[0], 0, 1)
    stream = forward_time(rows, time_weights, length, step)
    output, returned, channel_part = channel_layer(
        stream.reshape(model_size, seg_count, own, features), upstream, channel_weights, neighbors
    )
    series_grad, time_part = backward_time(
        rows, returned.reshape(length, own, features), time_weights, length, step
    )
    time_grads, channel_grads = reduce_grads(time_part, channel_part)
    return (
        jnp.swapaxes(output, 0, 1)[None],
        series_grad.reshape(series.shape),
        time_grads,
        channel_grads,
    )


def solution(mesh):
    placed = (P("dp", "mp", None, None), P("dp", None, "mp", None), P(), P(), P())
    return jax.shard_map(
        shards,
        mesh=mesh,
        in_specs=placed,
        out_specs=(
            P("dp", None, "mp", None),
            P("dp", "mp", None, None),
            P(None, "mp", None),
            P(None, "mp", None),
        ),
        check_vma=False,
    )
```
